32 devices in a mesh: groups: 2 (over y), cells: 4 (over z), nodes: 2 (over x), sub: 2 (over core).
Axes of the slice: x: 2, y: 2, z: 4, core: 2. Of those that a mesh axis runs over, the one named last changes fastest.
Arguments:
- adjoint_start: float32 [4, 5, 16384], P('nodes', None, ('groups', 'cells', 'sub')), parts along dimension 2, may hold values from -6 to 6
- adjoint_rhs: float32 [4, 5, 16384], P('nodes', None, ('groups', 'cells', 'sub')), parts along dimension 2, may hold values from -6 to 6
- off_blocks: bfloat16 [4, 6, 25, 16384], P('nodes', None, None, ('groups', 'cells', 'sub')), parts along dimension 3, may hold values from -0.5 to 0.5
- diag_inverse: float32 [4, 25, 16384], P('nodes', None, ('groups', 'cells', 'sub')), parts along dimension 2, may hold values from -2.4 to 2.4
- neighbours: int32 [6, 8192], P(None, ('cells', 'sub')), may hold values from -1 to 8191, as said below
- node_weights: float32 [4], P('nodes'), may hold values from 0.05 to 0.5
- sens_blocks: bfloat16 [4, 15, 16384], P('nodes', None, ('groups', 'cells', 'sub')), parts along dimension 2, may hold values from -1.796875 to 1.796875
- cell_points: float32 [3, 8192], P(None, ('cells', 'sub')), may hold values from 0 to 1
- base_points: float32 [3, 4096], replicated, may hold values from 0 to 1
- ffd_index: int32 [4096, 8], replicated, may hold values from 0 to 511
- ffd_weight: float32 [4096, 8], replicated, may hold values from 0 to 1
Outputs:
- adjoint: float32 [4, 5, 16384], P('nodes', None, ('groups', 'cells', 'sub')), parts along dimension 2
- control_grad: float32 [6, 512], P('groups'), parts along dimension 0
The draws below stay inside these ranges and needn't reach their ends.
There are 2 independent parts, one for each index of `groups`. The reference program is written for one: setup_inputs(seed, part) draws one part's arguments, and reference() takes and returns one part's arrays. A program takes and returns all parts, laid end to end along the dimension named above; an argument that names none is the same for every part. Nothing has to cross between parts.
Inputs may be any that keep to these rules, and one draw needn't show every extreme that they name: `neighbours`: each entry is -1 (no neighbour) or the index of a cell at most 1024 away from the cell; the distance 1024 occurs.
All inputs are finite; a program needn't handle non-finite values.
Results may differ from the reference program's by a relative error of at most 0.0003.
Values sent between devices are 32-bit elements; how exact they have to be, the bound alone decides.
A program may use at most 64 MiB of HBM per device.

```python
import math
import jax
import jax.numpy as jnp
from jax import lax

REACH = 1024
NODES = 4
NCELLS = 8192
FACES = 6
SWEEPS = 2
BASE = 4096
FFD = 512


def draw_neighbours(key, part):
    key_dist = jax.random.fold_in(key, 11)
    key_sign = jax.random.fold_in(key, 12)
    key_pad = jax.random.fold_in(key, 13)
    distance = jax.random.randint(key_dist, (FACES, NCELLS), 1, REACH + 1)
    upward = jax.random.randint(key_sign, (FACES, NCELLS), 0, 2)
    offset = jnp.where(upward == 1, distance, -distance)
    target = jnp.arange(NCELLS, dtype=jnp.int32)[None, :] + offset
    padded = jax.random.randint(key_pad, (FACES, NCELLS), 0, 6) == 0
    inside = (target >= 0) & (target < NCELLS)
    result = jnp.where(inside & jnp.logical_not(padded), target, -1).astype(jnp.int32)
    return result.at[0, REACH].set(0)


def touch_ends(values, rng, least, high):
    index_at = [jax.random.randint(jax.random.fold_in(rng, axis), (), 0, length) for axis, length in enumerate(values.shape)]
    main_axis = values.shape.index(max(values.shape))
    neighbour = index_at[:main_axis] + [(index_at[main_axis] + 1) % values.shape[main_axis]] + index_at[main_axis + 1:]
    return values.at[tuple(index_at)].set(least).at[tuple(neighbour)].set(high)


def block_scale(rng, dims, split, low, largest):
    level = 1.0
    for position, shards_of in split:
        steps = jax.random.uniform(jax.random.fold_in(jax.random.fold_in(rng, 6), position), (shards_of,), jnp.float32, low / len(split), largest / len(split))
        level = level * jnp.repeat(jnp.exp(steps), dims[position] // shards_of).reshape((-1,) + (1,) * (len(dims) - 1 - position))
    return level


def centred(stream_key, extent, scale, bound, cuts=(), kind=jnp.bfloat16):
    loudness = block_scale(stream_key, extent, cuts, -0.22, 0.18) if cuts else 1.0
    drawn = jax.random.normal(stream_key, extent, jnp.float32) * scale * loudness
    return jnp.minimum(jnp.maximum(drawn, -bound), bound).astype(kind)


def setup_inputs(seed: int = 0, part: int = 0) -> dict:
    key_of = jax.random.split(jax.random.key(seed), 12)
    part_splits = jax.random.split(jax.random.fold_in(key_of[11], part), 12)
    return {
        "adjoint_start": centred(part_splits[0], (NODES, 5, NCELLS), 1.0, 6.0, ((0, 2), (2, 8)), jnp.float32),
        "adjoint_rhs": centred(part_splits[1], (NODES, 5, NCELLS), 1.0, 6.0, ((0, 2), (2, 8)), jnp.float32),
        "off_blocks": centred(part_splits[2], (NODES, FACES, 25, NCELLS), 0.08, 0.5, ((0, 2), (3, 8))),
        "diag_inverse": centred(part_splits[3], (NODES, 25, NCELLS), 0.4, 2.4, ((0, 2), (2, 8)), jnp.float32),
        "neighbours": draw_neighbours(jax.random.fold_in(key_of[11], 71), part),
        "node_weights": jnp.clip(jnp.exp(math.log(0.5) - 2.3025851 * jax.random.uniform(key_of[5], (NODES,), jnp.float32) ** block_scale(key_of[5], (NODES,), ((0, 2),), -0.2, 0.2)), 0.05, 0.5),
        "sens_blocks": centred(part_splits[6], (NODES, 15, NCELLS), 0.3, 1.796875, ((0, 2), (2, 8))),
        "cell_points": jnp.clip(1.0 * jax.random.uniform(key_of[7], (3, NCELLS), jnp.float32) ** block_scale(key_of[7], (3, NCELLS), ((1, 8),), -0.2, 0.2), 0.0, 1.0),
        "base_points": jnp.clip(jax.random.uniform(key_of[8], (3, BASE), jnp.float32, 0.0, 1.0), 0.0, 1.0),
        "ffd_index": touch_ends(jax.random.randint(key_of[9], (BASE, 8), 0, FFD), jax.random.fold_in(key_of[9], 1), 0, FFD - 1).astype(jnp.int32),
        "ffd_weight": jnp.clip(jax.random.uniform(key_of[10], (BASE, 8), jnp.float32, 0.0, 1.0), 0.0, 1.0),
    }


support_radius = 0.3

def relax(adjoint, adjoint_rhs, off_blocks, diag_inverse, neighbours):
    present = neighbours >= 0
    index_safe = jnp.where(present, neighbours, 0)
    coupled = jnp.zeros(adjoint.shape, jnp.float32)
    node_count = adjoint.shape[0]
    for face_slot in range(FACES):
        beside = jnp.where(present[face_slot][None, None, :], adjoint[:, :, index_safe[face_slot]], 0.0)
        coupling = off_blocks[:, face_slot].astype(jnp.float32).reshape(node_count, 5, 5, -1)
        coupled = coupled + lax.optimization_barrier(jnp.sum(coupling * beside[:, None], axis=2))
    inverse = diag_inverse.reshape(node_count, 5, 5, -1)
    return lax.optimization_barrier(jnp.sum(inverse * (adjoint_rhs - coupled)[:, None], axis=2))

def kernel_sum(sensitivity, points, base):
    squared = jnp.zeros((points.shape[1], base.shape[1]), jnp.float32)
    for axis_slot in range(3):
        squared = squared + (points[axis_slot][:, None] - base[axis_slot][None, :]) ** 2
    ratio = jnp.sqrt(squared) / support_radius
    kernel = jnp.maximum(1.0 - ratio, 0.0) ** 4 * (4.0 * ratio + 1.0)
    return jnp.dot(sensitivity, kernel, precision=lax.Precision.HIGHEST, preferred_element_type=jnp.float32)

def lattice_matrix(lattice_index, lattice_weight, columns):
    matches = lattice_index[:, :, None] == jnp.arange(columns, dtype=jnp.int32)[None, None, :]
    return lax.optimization_barrier(jnp.sum(jnp.where(matches, lattice_weight[:, :, None], 0.0), axis=1))

def reference(adjoint_start, adjoint_rhs, off_blocks, diag_inverse, neighbours, node_weights, sens_blocks, cell_points, base_points, ffd_index, ffd_weight):
    adjoint = adjoint_start
    for sweep_step in range(SWEEPS):
        adjoint = relax(adjoint, adjoint_rhs, off_blocks, diag_inverse, neighbours)
    derive = sens_blocks.astype(jnp.float32).reshape(adjoint.shape[0], 5, 3, -1)
    per_node = lax.optimization_barrier(jnp.sum(adjoint[:, :, None] * derive, axis=1))
    sensitivity = lax.optimization_barrier(jnp.sum(node_weights[:, None, None] * per_node, axis=0))
    cell_block = min(4096, NCELLS)

    def add_block(block_index, carry):
        sens_part = lax.dynamic_slice_in_dim(sensitivity, block_index * cell_block, cell_block, 1)
        point_part = lax.dynamic_slice_in_dim(cell_points, block_index * cell_block, cell_block, 1)
        return carry + kernel_sum(sens_part, point_part, base_points)
    base_grad = lax.fori_loop(0, NCELLS // cell_block, add_block, jnp.zeros((3, BASE), jnp.float32))
    base_grad = base_grad / jnp.sqrt(jnp.float32(NCELLS))
    lattice = lattice_matrix(ffd_index, ffd_weight, FFD)
    control_grad = jnp.dot(base_grad, lattice, precision=lax.Precision.HIGHEST, preferred_element_type=jnp.float32)
    return (adjoint, control_grad)
```

```python
import functools

import jax
import jax.numpy as jnp
from jax import lax
from jax.experimental import pallas as pl
from jax.experimental.pallas import tpu as pltpu
from jax.sharding import PartitionSpec as P

SWEEPS = 2
FFD = 512
LANES = 128
ROWS = 8
TILE = 256

support_radius = 0.3
MESH = pl.DeviceIdType.MESH


def split2(x):
    hi = x.astype(jnp.bfloat16)
    return hi, (x - hi.astype(jnp.float32)).astype(jnp.bfloat16)


def split3(x):
    one = x.astype(jnp.bfloat16).astype(jnp.float32)
    two = (x - one).astype(jnp.bfloat16).astype(jnp.float32)
    return one, two, (x - one) - two


def kernel(
    scale,
    weight_ref,
    adj_ref,
    rhs_ref,
    nb_ref,
    sens_ref,
    point_ref,
    base_ref,
    ffd_index_ref,
    ffd_weight_ref,
    off_hbm,
    inv_hbm,
    out_ref,
    grad_ref,
    off_ref,
    inv_ref,
    wide,
    win,
    rel_ref,
    lane_ref,
    points,
    cell_feat,
    base_feat,
    k_hi,
    k_lo,
    l_hi,
    l_lo,
    sens_rows,
    sens_slots,
    sens_mat,
    grad_slots,
    load_sem,
    halo_send,
    halo_recv,
    point_send,
    point_recv,
    sens_send,
    sens_recv,
    grad_send,
    grad_recv,
):
    cells, subs, nodes = (lax.axis_size(a) for a in ("cells", "sub", "nodes"))
    cell_at, sub_at, node_at = (lax.axis_index(a) for a in ("cells", "sub", "nodes"))
    here, places = cell_at * subs + sub_at, cells * subs
    team, crew = node_at * subs + sub_at, nodes * subs
    me, everyone = cell_at * crew + team, cells * crew
    nodes_here = weight_ref.shape[0]
    rows = adj_ref.shape[1]
    blocks = rows // nodes_here
    cell_count = blocks * LANES
    base_own = base_feat.shape[1]

    def member(index):
        return {"nodes": index // subs, "sub": index % subs}

    def anyone(index):
        return dict(member(index % crew), cells=index // crew)

    barrier = pltpu.get_barrier_semaphore()
    for step in range(1, everyone):
        pl.semaphore_signal(
            barrier, inc=1, device_id=anyone((me + step) % everyone), device_id_type=MESH
        )
    off_load = pltpu.make_async_copy(off_hbm, off_ref, load_sem.at[0])
    inv_load = pltpu.make_async_copy(inv_hbm, inv_ref, load_sem.at[1])
    off_load.start()
    inv_load.start()

    wide[0, :, rows : 2 * rows, :] = adj_ref[...]

    first_cell = here * cell_count
    for face in range(nb_ref.shape[0]):
        for block in range(blocks):
            entry = nb_ref[face : face + 1, block * LANES : (block + 1) * LANES]
            local = entry - first_cell + cell_count
            chunk = jnp.where(entry >= 0, (local >> 7) - block, -1)
            span = pl.ds(block * nodes_here, nodes_here)
            rel_ref[face, span, :] = jnp.broadcast_to(chunk, (nodes_here, LANES))
            lane_ref[face, span, :] = jnp.broadcast_to(local & (LANES - 1), (nodes_here, LANES))

    base_start = team * base_own

    def build_lattice(step, carry):
        source = pl.ds(pl.multiple_of(base_start + step * LANES, LANES), LANES)
        target = pl.ds(pl.multiple_of(step * LANES, LANES), LANES)
        index = ffd_index_ref[:, source]
        weight = ffd_weight_ref[:, source]
        group = 64
        row = lax.broadcasted_iota(jnp.int32, (group, LANES), 0)
        for top in range(0, FFD, group):
            total = jnp.zeros((group, LANES), jnp.float32)
            for slot in range(index.shape[0]):
                match = row == index[slot : slot + 1, :] - top
                total = total + jnp.where(match, weight[slot : slot + 1, :], 0.0)
            hi, lo = split2(total)
            l_hi[top : top + group, target] = hi
            l_lo[top : top + group, target] = lo
        return carry

    lax.fori_loop(0, base_own // LANES, build_lattice, 0)

    @pl.when(here == 0)
    def _():
        wide[:, :, 0:rows, :] = jnp.zeros((SWEEPS, 5, rows, LANES), jnp.float32)

    @pl.when(here == places - 1)
    def _():
        wide[:, :, 2 * rows : 3 * rows, :] = jnp.zeros((SWEEPS, 5, rows, LANES), jnp.float32)

    pl.semaphore_wait(barrier, everyone - 1)

    def halo(sweep, side):
        other = here + 1 if side == 0 else here - 1
        start = 0 if side == 0 else 2 * rows
        return pltpu.make_async_remote_copy(
            src_ref=wide.at[sweep, :, pl.ds(rows, rows), :],
            dst_ref=wide.at[sweep, :, pl.ds(start, rows), :],
            send_sem=halo_send.at[sweep, side],
            recv_sem=halo_recv.at[sweep, side],
            device_id={"cells": other // subs, "sub": other % subs},
            device_id_type=MESH,
        )

    def halo_start(sweep):
        @pl.when(here < places - 1)
        def _():
            halo(sweep, 0).start()

        @pl.when(here > 0)
        def _():
            halo(sweep, 1).start()

    def halo_wait(sweep):
        @pl.when(here > 0)
        def _():
            halo(sweep, 0).wait_recv()

        @pl.when(here < places - 1)
        def _():
            halo(sweep, 1).wait_recv()

    def halo_sent(sweep):
        @pl.when(here < places - 1)
        def _():
            halo(sweep, 0).wait_send()

        @pl.when(here > 0)
        def _():
            halo(sweep, 1).wait_send()

    def point_copy(step):
        return pltpu.make_async_remote_copy(
            src_ref=point_ref,
            dst_ref=points.at[step],
            send_sem=point_send.at[step],
            recv_sem=point_recv.at[step],
            device_id={"sub": (sub_at + step) % subs},
            device_id_type=MESH,
        )

    halo_start(0)
    for step in range(1, subs):
        point_copy(step).start()

    def features(ref, at, xyz, own):
        one, two, three = split3(xyz)
        square = xyz[0:1] * xyz[0:1] + xyz[1:2] * xyz[1:2] + xyz[2:3] * xyz[2:3]
        pieces = [one, one, two, two, one, three] if own else [one, two, one, two, three, one]
        for slot, piece in enumerate(pieces):
            ref[3 * slot : 3 * slot + 3, at] = piece if own else -2.0 * piece
        parts = split3(square)
        for slot in range(3):
            ones = jnp.ones_like(square)
            ref[18 + slot : 19 + slot, at] = parts[slot] if own else ones
            ref[21 + slot : 22 + slot, at] = ones if own else parts[slot]

    inverse_radius = 1.0 / support_radius
    base_xyz = base_ref[:, pl.ds(pl.multiple_of(base_start, LANES), base_own)]
    features(base_feat, slice(None), (base_xyz - 0.5) * inverse_radius, False)

    def build_kernel(step):
        xyz = point_ref[...] if step == 0 else points[step]
        features(cell_feat, slice(None), (xyz - 0.5) * inverse_radius, True)

        def tile(index, carry):
            source = pl.ds(pl.multiple_of(index * TILE, TILE), TILE)
            target = pl.ds(pl.multiple_of(step * cell_count + index * TILE, TILE), TILE)
            mine = cell_feat[:, source].T.astype(jnp.bfloat16)
            for left in range(0, base_own, TILE):
                other = base_feat[:, left : left + TILE].astype(jnp.bfloat16)
                squared = jnp.dot(mine, other, preferred_element_type=jnp.float32)
                squared = jnp.maximum(squared, 1e-20)
                ratio = squared * lax.rsqrt(squared)
                inside = jnp.maximum(1.0 - ratio, 0.0)
                inside = inside * inside
                value = inside * inside * (4.0 * ratio + 1.0)
                hi, lo = split2(value)
                k_hi[target, left : left + TILE] = hi
                k_lo[target, left : left + TILE] = lo
            return carry

        lax.fori_loop(0, cell_count // TILE, tile, 0)

    def relax(sweep):
        stride = ROWS // nodes_here
        for start in range(win.shape[0]):
            for comp in range(5):
                at = start * nodes_here
                win[start, comp] = wide[sweep, comp, at : at + ROWS, :]

        def face_step(face, coupled):
            beside = [[] for _ in range(5)]
            for piece in range(rows // ROWS):
                span = slice(piece * ROWS, (piece + 1) * ROWS)
                rel, lane = rel_ref[face, span, :], lane_ref[face, span, :]
                found = [jnp.zeros((ROWS, LANES), jnp.float32)] * 5
                for chunk in range(2 * blocks + 1):
                    match = rel == chunk
                    for comp in range(5):
                        taken = jnp.take_along_axis(
                            win[chunk + stride * piece, comp], lane, axis=1
                        )
                        found[comp] = jnp.where(match, taken, found[comp])
                for comp in range(5):
                    beside[comp].append(found[comp])
            beside = [jnp.concatenate(part, axis=0) for part in beside]
            coupled = list(coupled)
            for a in range(5):
                for b in range(5):
                    block = off_ref[face, 5 * a + b].astype(jnp.float32)
                    coupled[a] = coupled[a] + block * beside[b]
            return tuple(coupled)

        zero = jnp.zeros((rows, LANES), jnp.float32)
        coupled = lax.fori_loop(0, off_ref.shape[0], face_step, (zero,) * 5)
        if sweep == 0:
            inv_load.wait()
        rest = [rhs_ref[b] - coupled[b] for b in range(5)]
        result = []
        for a in range(5):
            total = inv_ref[5 * a] * rest[0]
            for b in range(1, 5):
                total = total + inv_ref[5 * a + b] * rest[b]
            result.append(total)
        return result

    build_kernel(0)
    halo_wait(0)
    off_load.wait()
    first = relax(0)
    for a in range(5):
        wide[1, a, rows : 2 * rows, :] = first[a]
    halo_start(1)
    for step in range(1, subs):
        point_copy(step).wait_recv()
        build_kernel(step)
    halo_wait(1)
    adjoint = relax(1)
    for a in range(5):
        out_ref[a] = adjoint[a]

    for k in range(3):
        total = adjoint[0] * sens_ref[k].astype(jnp.float32)
        for a in range(1, 5):
            total = total + adjoint[a] * sens_ref[3 * a + k].astype(jnp.float32)
        sens_rows[k] = total
    for k in range(3):
        total = weight_ref[0] * sens_rows[k, pl.ds(0, blocks, stride=nodes_here), :]
        for n in range(1, nodes_here):
            total = total + weight_ref[n] * sens_rows[k, pl.ds(n, blocks, stride=nodes_here), :]
        sens_slots[team, k] = total

    def sens_copy(step):
        return pltpu.make_async_remote_copy(
            src_ref=sens_slots.at[team],
            dst_ref=sens_slots.at[team],
            send_sem=sens_send.at[step],
            recv_sem=sens_recv.at[team],
            device_id=member((team + step) % crew),
            device_id_type=MESH,
        )

    def sens_arrival(step):
        slot = (team + step) % crew
        return pltpu.make_async_remote_copy(
            src_ref=sens_slots.at[slot],
            dst_ref=sens_slots.at[slot],
            send_sem=sens_send.at[step],
            recv_sem=sens_recv.at[slot],
            device_id=member((team + step) % crew),
            device_id_type=MESH,
        )

    for step in range(1, crew):
        sens_copy(step).start()
    sens_mat[...] = jnp.zeros_like(sens_mat)
    for step in range(1, crew):
        sens_arrival(step).wait_recv()
    for step in range(subs):
        whose = (sub_at - step + subs) % subs
        for k in range(3):
            total = sens_slots[whose, k]
            for n in range(1, nodes):
                total = total + sens_slots[n * subs + whose, k]
            hi = total.astype(jnp.bfloat16).astype(jnp.float32)
            lo = total - hi
            for block in range(blocks):
                at = step * cell_count + block * LANES
                sens_mat[k : k + 1, at : at + LANES] = hi[block : block + 1, :]
                sens_mat[ROWS + k : ROWS + k + 1, at : at + LANES] = lo[block : block + 1, :]

    left = sens_mat[...].astype(jnp.bfloat16)
    product = jnp.dot(left, k_hi[...], preferred_element_type=jnp.float32)
    product = product + jnp.dot(left, k_lo[...], preferred_element_type=jnp.float32)
    base_grad = (product[0:ROWS] + product[ROWS:]) * scale
    hi = base_grad.astype(jnp.bfloat16).astype(jnp.float32)
    left = jnp.concatenate([hi, base_grad - hi], axis=0).astype(jnp.bfloat16)
    contract = (((1,), (1,)), ((), ()))
    product = lax.dot_general(left, l_hi[...], contract, preferred_element_type=jnp.float32)
    product = product + lax.dot_general(
        left, l_lo[...], contract, preferred_element_type=jnp.float32
    )
    own = product[0:ROWS] + product[ROWS:]
    for block in range(FFD // LANES):
        grad_slots[me, 3 * block : 3 * block + 3, :] = own[
            0:3, block * LANES : (block + 1) * LANES
        ]

    def grad_copy(step, slot):
        return pltpu.make_async_remote_copy(
            src_ref=grad_slots.at[slot],
            dst_ref=grad_slots.at[slot],
            send_sem=grad_send.at[step],
            recv_sem=grad_recv.at[slot],
            device_id=anyone((me + step) % everyone),
            device_id_type=MESH,
        )

    for step in range(1, everyone):
        grad_copy(step, me).start()
    halo_sent(0)
    halo_sent(1)
    for step in range(1, subs):
        point_copy(step).wait_send()
    for step in range(1, crew):
        sens_copy(step).wait_send()
    for step in range(1, everyone):
        grad_copy(step, (me + step) % everyone).wait_recv()
    total = grad_slots[0]
    for slot in range(1, everyone):
        total = total + grad_slots[slot]
    for block in range(FFD // LANES):
        grad_ref[:, block * LANES : (block + 1) * LANES] = total[3 * block : 3 * block + 3, :]
    for step in range(1, everyone):
        grad_copy(step, me).wait_send()


def to_rows(array):
    array = jnp.moveaxis(array, 0, -2)
    lead, (nodes, cells) = array.shape[:-2], array.shape[-2:]
    array = array.reshape(lead + (nodes, cells // LANES, LANES))
    array = jnp.swapaxes(array, -3, -2)
    return array.reshape(lead + (nodes * cells // LANES, LANES))


def from_rows(array, nodes):
    lead, rows = array.shape[:-2], array.shape[-2]
    array = array.reshape(lead + (rows // nodes, nodes, LANES))
    array = jnp.swapaxes(array, -3, -2).reshape(lead + (nodes, rows // nodes * LANES))
    return jnp.moveaxis(array, -2, 0)


def body(
    adjoint_start,
    adjoint_rhs,
    off_blocks,
    diag_inverse,
    neighbours,
    node_weights,
    sens_blocks,
    cell_points,
    base_points,
    ffd_index,
    ffd_weight,
):
    nodes_here, _, cell_count = adjoint_start.shape
    faces = off_blocks.shape[1]
    cells, subs, nodes = (lax.axis_size(a) for a in ("cells", "sub", "nodes"))
    crew = nodes * subs
    everyone = cells * crew
    blocks = cell_count // LANES
    rows = blocks * nodes_here
    base_own = base_points.shape[1] // crew
    windows = 2 * blocks + 1 + (rows // ROWS - 1) * (ROWS // nodes_here)
    scale = 1.0 / float(cell_count * cells * subs) ** 0.5
    vmem = pl.BlockSpec(memory_space=pltpu.VMEM)
    hbm = pl.BlockSpec(memory_space=pl.ANY)
    f32, bf16 = jnp.float32, jnp.bfloat16
    dma = pltpu.SemaphoreType.DMA
    off_rows, inv_rows = to_rows(off_blocks), to_rows(diag_inverse)
    adjoint, control = pl.pallas_call(
        functools.partial(kernel, scale),
        out_shape=(
            jax.ShapeDtypeStruct((5, rows, LANES), f32),
            jax.ShapeDtypeStruct((3, FFD), f32),
        ),
        in_specs=[pl.BlockSpec(memory_space=pltpu.SMEM)] + [vmem] * 8 + [hbm] * 2,
        out_specs=(vmem, vmem),
        scratch_shapes=[
            pltpu.VMEM(off_rows.shape, bf16),
            pltpu.VMEM(inv_rows.shape, f32),
            pltpu.VMEM((SWEEPS, 5, 3 * rows, LANES), f32),
            pltpu.VMEM((windows, 5, ROWS, LANES), f32),
            pltpu.VMEM((faces, rows, LANES), jnp.int32),
            pltpu.VMEM((faces, rows, LANES), jnp.int32),
            pltpu.VMEM((subs, 3, cell_count), f32),
            pltpu.VMEM((24, cell_count), f32),
            pltpu.VMEM((24, base_own), f32),
            pltpu.VMEM((subs * cell_count, base_own), bf16),
            pltpu.VMEM((subs * cell_count, base_own), bf16),
            pltpu.VMEM((FFD, base_own), bf16),
            pltpu.VMEM((FFD, base_own), bf16),
            pltpu.VMEM((3, rows, LANES), f32),
            pltpu.VMEM((crew, 3, blocks, LANES), f32),
            pltpu.VMEM((2 * ROWS, subs * cell_count), f32),
            pltpu.VMEM((everyone, 3 * FFD // LANES, LANES), f32),
            dma((2,)),
            dma((SWEEPS, 2)),
            dma((SWEEPS, 2)),
            dma((subs,)),
            dma((subs,)),
            dma((crew,)),
            dma((crew,)),
            dma((everyone,)),
            dma((everyone,)),
        ],
        compiler_params=pltpu.CompilerParams(
            collective_id=0, has_side_effects=True, vmem_limit_bytes=60 * 1024 * 1024
        ),
    )(
        node_weights,
        to_rows(adjoint_start),
        to_rows(adjoint_rhs),
        neighbours,
        to_rows(sens_blocks),
        cell_points,
        base_points,
        ffd_index.T,
        ffd_weight.T,
        off_rows,
        inv_rows,
    )
    return from_rows(adjoint, nodes_here), control


def solution(mesh):
    return jax.shard_map(
        body,
        mesh=mesh,
        in_specs=(
            P("nodes", None, ("groups", "cells", "sub")),
            P("nodes", None, ("groups", "cells", "sub")),
            P("nodes", None, None, ("groups", "cells", "sub")),
            P("nodes", None, ("groups", "cells", "sub")),
            P(None, ("cells", "sub")),
            P("nodes"),
            P("nodes", None, ("groups", "cells", "sub")),
            P(None, ("cells", "sub")),
            P(),
            P(),
            P(),
        ),
        out_specs=(P("nodes", None, ("groups", "cells", "sub")), P("groups", None)),
        check_vma=False,
    )
```

```python
import functools

import jax
import jax.numpy as jnp
from jax import lax
from jax.experimental import pallas as pl
from jax.experimental.pallas import tpu as pltpu
from jax.sharding import PartitionSpec as P

SWEEPS = 2
FFD = 512
LANES = 128
ROWS = 8
TILE = 256

support_radius = 0.3
MESH = pl.DeviceIdType.MESH


def split2(x):
    hi = x.astype(jnp.bfloat16)
    return hi, (x - hi.astype(jnp.float32)).astype(jnp.bfloat16)


def split3(x):
    one = x.astype(jnp.bfloat16).astype(jnp.float32)
    two = (x - one).astype(jnp.bfloat16).astype(jnp.float32)
    return one, two, (x - one) - two


def kernel(
    scale,
    weight_ref,
    adj_hbm,
    point_hbm,
    nb_hbm,
    base_hbm,
    off_hbm,
    rhs_hbm,
    inv_hbm,
    sens_hbm,
    ffd_index_hbm,
    ffd_weight_hbm,
    out_ref,
    grad_ref,
    point_ref,
    nb_ref,
    base_ref,
    off_ref,
    rhs_ref,
    inv_ref,
    sens_ref,
    ffd_index_ref,
    ffd_weight_ref,
    wide,
    win,
    rel_ref,
    lane_ref,
    points,
    cell_feat,
    base_feat,
    k_hi,
    k_lo,
    l_hi,
    l_lo,
    sens_rows,
    sens_slots,
    sens_mat,
    grad_slots,
    load_sem,
    halo_send,
    halo_recv,
    point_send,
    point_recv,
    sens_send,
    sens_recv,
    grad_send,
    grad_recv,
    known,
):
    cells, subs, nodes = (lax.axis_size(a) for a in ("cells", "sub", "nodes"))
    cell_at, sub_at, node_at = (lax.axis_index(a) for a in ("cells", "sub", "nodes"))
    here, places = cell_at * subs + sub_at, cells * subs
    team, crew = node_at * subs + sub_at, nodes * subs
    me, everyone = cell_at * crew + team, cells * crew
    nodes_here = weight_ref.shape[0]
    rows = adj_hbm.shape[1]
    blocks = rows // nodes_here
    cell_count = blocks * LANES
    base_own = base_feat.shape[1]

    def member(index):
        return {"nodes": index // subs, "sub": index % subs}

    def anyone(index):
        return dict(member(index % crew), cells=index // crew)

    lower, upper = cell_at > 0, cell_at < cells - 1
    below, above = cell_at - 1, cell_at + 1

    barrier = pltpu.get_barrier_semaphore()

    def greet(device):
        pl.semaphore_signal(barrier, inc=1, device_id=device, device_id_type=MESH)

    greeted = crew - 1
    for step in range(1, crew):
        greet(member((team + step) % crew))
    greetings = [(lower, {"cells": below}), (upper, {"cells": above})]
    if subs > 1:
        first, last = sub_at == 0, sub_at == subs - 1
        greetings.append((jnp.logical_and(lower, first), {"cells": below, "sub": subs - 1}))
        greetings.append((jnp.logical_and(upper, last), {"cells": above, "sub": 0}))
    for exists, device in greetings:
        pl.when(exists)(functools.partial(greet, device))
        greeted = greeted + exists.astype(jnp.int32)

    base_start = pl.multiple_of(team * base_own, LANES)
    share = pl.ds(base_start, base_own)
    sources = (
        (adj_hbm, wide.at[0, :, pl.ds(rows, rows), :]),
        (point_hbm, point_ref),
        (nb_hbm, nb_ref),
        (base_hbm.at[:, share], base_ref),
        (off_hbm, off_ref),
        (rhs_hbm, rhs_ref),
        (inv_hbm, inv_ref),
        (sens_hbm, sens_ref),
        (ffd_index_hbm.at[:, share], ffd_index_ref),
        (ffd_weight_hbm.at[:, share], ffd_weight_ref),
    )
    loads = [
        pltpu.make_async_copy(source, target, load_sem.at[slot])
        for slot, (source, target) in enumerate(sources)
    ]
    for load in loads:
        load.start()
    (adj_load, point_load, nb_load, base_load, off_load, rhs_load, inv_load, sens_load) = loads[:8]

    def tell(stage):
        for side, (exists, other) in enumerate(((upper, above), (lower, below))):

            @pl.when(exists)
            def _():
                pl.semaphore_signal(
                    known.at[stage, side],
                    inc=1,
                    device_id={"cells": other},
                    device_id_type=MESH,
                )

    def hear(stage):
        for side, exists in enumerate((lower, upper)):

            @pl.when(exists)
            def _():
                pl.semaphore_wait(known.at[stage, side], 1)

    nb_load.wait()
    first_cell = here * cell_count
    for face in range(nb_ref.shape[0]):
        for block in range(blocks):
            entry = nb_ref[face : face + 1, block * LANES : (block + 1) * LANES]
            local = entry - first_cell + cell_count
            chunk = jnp.where(entry >= 0, (local >> 7) - block, -1)
            span = pl.ds(block * nodes_here, nodes_here)
            rel_ref[face, span, :] = jnp.broadcast_to(chunk, (nodes_here, LANES))
            lane_ref[face, span, :] = jnp.broadcast_to(local & (LANES - 1), (nodes_here, LANES))

    def build_lattice(step, carry):
        target = pl.ds(pl.multiple_of(step * LANES, LANES), LANES)
        index = ffd_index_ref[:, target]
        weight = ffd_weight_ref[:, target]
        group = 64
        row = lax.broadcasted_iota(jnp.int32, (group, LANES), 0)
        for top in range(0, FFD, group):
            total = jnp.zeros((group, LANES), jnp.float32)
            for slot in range(index.shape[0]):
                match = row == index[slot : slot + 1, :] - top
                total = total + jnp.where(match, weight[slot : slot + 1, :], 0.0)
            hi, lo = split2(total)
            l_hi[top : top + group, target] = hi
            l_lo[top : top + group, target] = lo
        return carry


    @pl.when(here == 0)
    def _():
        wide[:, :, 0:rows, :] = jnp.zeros((SWEEPS, 5, rows, LANES), jnp.float32)

    @pl.when(here == places - 1)
    def _():
        wide[:, :, 2 * rows : 3 * rows, :] = jnp.zeros((SWEEPS, 5, rows, LANES), jnp.float32)

    adj_load.wait()
    point_load.wait()
    pl.semaphore_wait(barrier, greeted)

    def halo(sweep, side):
        other = here + 1 if side == 0 else here - 1
        start = 0 if side == 0 else 2 * rows
        return pltpu.make_async_remote_copy(
            src_ref=wide.at[sweep, :, pl.ds(rows, rows), :],
            dst_ref=wide.at[sweep, :, pl.ds(start, rows), :],
            send_sem=halo_send.at[sweep, side],
            recv_sem=halo_recv.at[sweep, side],
            device_id={"cells": other // subs, "sub": other % subs},
            device_id_type=MESH,
        )

    def halo_start(sweep):
        @pl.when(here < places - 1)
        def _():
            halo(sweep, 0).start()

        @pl.when(here > 0)
        def _():
            halo(sweep, 1).start()

    def halo_wait(sweep):
        @pl.when(here > 0)
        def _():
            halo(sweep, 0).wait_recv()

        @pl.when(here < places - 1)
        def _():
            halo(sweep, 1).wait_recv()

    def halo_sent(sweep):
        @pl.when(here < places - 1)
        def _():
            halo(sweep, 0).wait_send()

        @pl.when(here > 0)
        def _():
            halo(sweep, 1).wait_send()

    def point_copy(step):
        return pltpu.make_async_remote_copy(
            src_ref=point_ref,
            dst_ref=points.at[step],
            send_sem=point_send.at[step],
            recv_sem=point_recv.at[step],
            device_id={"sub": (sub_at + step) % subs},
            device_id_type=MESH,
        )

    halo_start(0)
    for step in range(1, subs):
        point_copy(step).start()
    tell(0)
    base_load.wait()

    def features(ref, at, xyz, own):
        one, two, three = split3(xyz)
        square = xyz[0:1] * xyz[0:1] + xyz[1:2] * xyz[1:2] + xyz[2:3] * xyz[2:3]
        pieces = [one, one, two, two, one, three] if own else [one, two, one, two, three, one]
        for slot, piece in enumerate(pieces):
            ref[3 * slot : 3 * slot + 3, at] = piece if own else -2.0 * piece
        parts = split3(square)
        for slot in range(3):
            ones = jnp.ones_like(square)
            ref[18 + slot : 19 + slot, at] = parts[slot] if own else ones
            ref[21 + slot : 22 + slot, at] = ones if own else parts[slot]

    inverse_radius = 1.0 / support_radius
    features(base_feat, slice(None), (base_ref[...] - 0.5) * inverse_radius, False)

    def build_kernel(step):
        xyz = point_ref[...] if step == 0 else points[step]
        features(cell_feat, slice(None), (xyz - 0.5) * inverse_radius, True)

        def tile(index, carry):
            source = pl.ds(pl.multiple_of(index * TILE, TILE), TILE)
            target = pl.ds(pl.multiple_of(step * cell_count + index * TILE, TILE), TILE)
            mine = cell_feat[:, source].T.astype(jnp.bfloat16)
            for left in range(0, base_own, TILE):
                other = base_feat[:, left : left + TILE].astype(jnp.bfloat16)
                squared = jnp.dot(mine, other, preferred_element_type=jnp.float32)
                squared = jnp.maximum(squared, 1e-20)
                ratio = squared * lax.rsqrt(squared)
                inside = jnp.maximum(1.0 - ratio, 0.0)
                inside = inside * inside
                value = inside * inside * (4.0 * ratio + 1.0)
                hi, lo = split2(value)
                k_hi[target, left : left + TILE] = hi
                k_lo[target, left : left + TILE] = lo
            return carry

        lax.fori_loop(0, cell_count // TILE, tile, 0)

    def relax(sweep):
        stride = ROWS // nodes_here
        for start in range(win.shape[0]):
            for comp in range(5):
                at = start * nodes_here
                win[start, comp] = wide[sweep, comp, at : at + ROWS, :]

        def face_step(face, coupled):
            beside = [[] for _ in range(5)]
            for piece in range(rows // ROWS):
                span = slice(piece * ROWS, (piece + 1) * ROWS)
                rel, lane = rel_ref[face, span, :], lane_ref[face, span, :]
                found = [jnp.zeros((ROWS, LANES), jnp.float32)] * 5
                for chunk in range(2 * blocks + 1):
                    match = rel == chunk
                    for comp in range(5):
                        taken = jnp.take_along_axis(
                            win[chunk + stride * piece, comp], lane, axis=1
                        )
                        found[comp] = jnp.where(match, taken, found[comp])
                for comp in range(5):
                    beside[comp].append(found[comp])
            beside = [jnp.concatenate(part, axis=0) for part in beside]
            coupled = list(coupled)
            for a in range(5):
                for b in range(5):
                    block = off_ref[face, 5 * a + b].astype(jnp.float32)
                    coupled[a] = coupled[a] + block * beside[b]
            return tuple(coupled)

        zero = jnp.zeros((rows, LANES), jnp.float32)
        coupled = lax.fori_loop(0, off_ref.shape[0], face_step, (zero,) * 5)
        if sweep == 0:
            rhs_load.wait()
            inv_load.wait()
        rest = [rhs_ref[b] - coupled[b] for b in range(5)]
        result = []
        for a in range(5):
            total = inv_ref[5 * a] * rest[0]
            for b in range(1, 5):
                total = total + inv_ref[5 * a + b] * rest[b]
            result.append(total)
        return result

    build_kernel(0)
    halo_wait(0)
    off_load.wait()
    first = relax(0)
    for a in range(5):
        wide[1, a, rows : 2 * rows, :] = first[a]
    halo_start(1)
    if cells > 2:
        hear(0)
        tell(1)
    for step in range(1, subs):
        point_copy(step).wait_recv()
        build_kernel(step)
    halo_wait(1)
    adjoint = relax(1)
    for a in range(5):
        out_ref[a] = adjoint[a]

    sens_load.wait()
    for k in range(3):
        total = adjoint[0] * sens_ref[k].astype(jnp.float32)
        for a in range(1, 5):
            total = total + adjoint[a] * sens_ref[3 * a + k].astype(jnp.float32)
        sens_rows[k] = total
    for k in range(3):
        total = weight_ref[0] * sens_rows[k, pl.ds(0, blocks, stride=nodes_here), :]
        for n in range(1, nodes_here):
            total = total + weight_ref[n] * sens_rows[k, pl.ds(n, blocks, stride=nodes_here), :]
        sens_slots[team, k] = total

    def sens_copy(step):
        return pltpu.make_async_remote_copy(
            src_ref=sens_slots.at[team],
            dst_ref=sens_slots.at[team],
            send_sem=sens_send.at[step],
            recv_sem=sens_recv.at[team],
            device_id=member((team + step) % crew),
            device_id_type=MESH,
        )

    def sens_arrival(step):
        slot = (team + step) % crew
        return pltpu.make_async_remote_copy(
            src_ref=sens_slots.at[slot],
            dst_ref=sens_slots.at[slot],
            send_sem=sens_send.at[step],
            recv_sem=sens_recv.at[slot],
            device_id=member((team + step) % crew),
            device_id_type=MESH,
        )

    for step in range(1, crew):
        sens_copy(step).start()
    for stage in range(2, cells - 1):
        hear(stage - 1)
        tell(stage)
    sens_mat[...] = jnp.zeros_like(sens_mat)
    loads[8].wait()
    loads[9].wait()
    lax.fori_loop(0, base_own // LANES, build_lattice, 0)
    for step in range(1, crew):
        sens_arrival(step).wait_recv()
    for step in range(subs):
        whose = (sub_at - step + subs) % subs
        for k in range(3):
            total = sens_slots[whose, k]
            for n in range(1, nodes):
                total = total + sens_slots[n * subs + whose, k]
            hi = total.astype(jnp.bfloat16).astype(jnp.float32)
            lo = total - hi
            for block in range(blocks):
                at = step * cell_count + block * LANES
                sens_mat[k : k + 1, at : at + LANES] = hi[block : block + 1, :]
                sens_mat[ROWS + k : ROWS + k + 1, at : at + LANES] = lo[block : block + 1, :]

    left = sens_mat[...].astype(jnp.bfloat16)
    product = jnp.dot(left, k_hi[...], preferred_element_type=jnp.float32)
    product = product + jnp.dot(left, k_lo[...], preferred_element_type=jnp.float32)
    base_grad = (product[0:ROWS] + product[ROWS:]) * scale
    hi = base_grad.astype(jnp.bfloat16).astype(jnp.float32)
    left = jnp.concatenate([hi, base_grad - hi], axis=0).astype(jnp.bfloat16)
    contract = (((1,), (1,)), ((), ()))
    product = lax.dot_general(left, l_hi[...], contract, preferred_element_type=jnp.float32)
    product = product + lax.dot_general(
        left, l_lo[...], contract, preferred_element_type=jnp.float32
    )
    own = product[0:ROWS] + product[ROWS:]
    for block in range(FFD // LANES):
        grad_slots[me, 3 * block : 3 * block + 3, :] = own[
            0:3, block * LANES : (block + 1) * LANES
        ]

    def grad_copy(step, slot):
        return pltpu.make_async_remote_copy(
            src_ref=grad_slots.at[slot],
            dst_ref=grad_slots.at[slot],
            send_sem=grad_send.at[step],
            recv_sem=grad_recv.at[slot],
            device_id=anyone((me + step) % everyone),
            device_id_type=MESH,
        )

    if cells > 1:
        hear(cells - 2)
    for step in range(1, everyone):
        grad_copy(step, me).start()
    halo_sent(0)
    halo_sent(1)
    for step in range(1, subs):
        point_copy(step).wait_send()
    for step in range(1, crew):
        sens_copy(step).wait_send()
    for step in range(1, everyone):
        grad_copy(step, (me + step) % everyone).wait_recv()
    total = grad_slots[0]
    for slot in range(1, everyone):
        total = total + grad_slots[slot]
    for block in range(FFD // LANES):
        grad_ref[:, block * LANES : (block + 1) * LANES] = total[3 * block : 3 * block + 3, :]
    for step in range(1, everyone):
        grad_copy(step, me).wait_send()


def finish(adjoint_in, control_in, adjoint_out, control_out):
    adjoint_out[...] = adjoint_in[...]
    control_out[...] = control_in[...]


def to_rows(array):
    array = jnp.moveaxis(array, 0, -2)
    lead, (nodes, cells) = array.shape[:-2], array.shape[-2:]
    array = array.reshape(lead + (nodes, cells // LANES, LANES))
    array = jnp.swapaxes(array, -3, -2)
    return array.reshape(lead + (nodes * cells // LANES, LANES))


def from_rows(array, nodes):
    lead, rows = array.shape[:-2], array.shape[-2]
    array = array.reshape(lead + (rows // nodes, nodes, LANES))
    array = jnp.swapaxes(array, -3, -2).reshape(lead + (nodes, rows // nodes * LANES))
    return jnp.moveaxis(array, -2, 0)


def body(
    adjoint_start,
    adjoint_rhs,
    off_blocks,
    diag_inverse,
    neighbours,
    node_weights,
    sens_blocks,
    cell_points,
    base_points,
    ffd_index,
    ffd_weight,
):
    nodes_here, _, cell_count = adjoint_start.shape
    faces = off_blocks.shape[1]
    cells, subs, nodes = (lax.axis_size(a) for a in ("cells", "sub", "nodes"))
    crew = nodes * subs
    everyone = cells * crew
    blocks = cell_count // LANES
    rows = blocks * nodes_here
    base_own = base_points.shape[1] // crew
    windows = 2 * blocks + 1 + (rows // ROWS - 1) * (ROWS // nodes_here)
    scale = 1.0 / float(cell_count * cells * subs) ** 0.5
    vmem = pl.BlockSpec(memory_space=pltpu.VMEM)
    hbm = pl.BlockSpec(memory_space=pltpu.HBM)
    f32, bf16 = jnp.float32, jnp.bfloat16
    dma = pltpu.SemaphoreType.DMA
    off_rows, inv_rows = to_rows(off_blocks), to_rows(diag_inverse)
    sens_cells = to_rows(sens_blocks)
    adjoint, control = pl.pallas_call(
        functools.partial(kernel, scale),
        out_shape=(
            jax.ShapeDtypeStruct((5, rows, LANES), f32),
            jax.ShapeDtypeStruct((3, FFD), f32),
        ),
        in_specs=[pl.BlockSpec(memory_space=pltpu.SMEM)] + [hbm] * 10,
        out_specs=(vmem, vmem),
        scratch_shapes=[
            pltpu.VMEM(cell_points.shape, f32),
            pltpu.VMEM(neighbours.shape, jnp.int32),
            pltpu.VMEM((3, base_own), f32),
            pltpu.VMEM(off_rows.shape, bf16),
            pltpu.VMEM((5, rows, LANES), f32),
            pltpu.VMEM(inv_rows.shape, f32),
            pltpu.VMEM(sens_cells.shape, bf16),
            pltpu.VMEM((ffd_index.shape[1], base_own), jnp.int32),
            pltpu.VMEM((ffd_index.shape[1], base_own), f32),
            pltpu.VMEM((SWEEPS, 5, 3 * rows, LANES), f32),
            pltpu.VMEM((windows, 5, ROWS, LANES), f32),
            pltpu.VMEM((faces, rows, LANES), jnp.int32),
            pltpu.VMEM((faces, rows, LANES), jnp.int32),
            pltpu.VMEM((subs, 3, cell_count), f32),
            pltpu.VMEM((24, cell_count), f32),
            pltpu.VMEM((24, base_own), f32),
            pltpu.VMEM((subs * cell_count, base_own), bf16),
            pltpu.VMEM((subs * cell_count, base_own), bf16),
            pltpu.VMEM((FFD, base_own), bf16),
            pltpu.VMEM((FFD, base_own), bf16),
            pltpu.VMEM((3, rows, LANES), f32),
            pltpu.VMEM((crew, 3, blocks, LANES), f32),
            pltpu.VMEM((2 * ROWS, subs * cell_count), f32),
            pltpu.VMEM((everyone, 3 * FFD // LANES, LANES), f32),
            dma((10,)),
            dma((SWEEPS, 2)),
            dma((SWEEPS, 2)),
            dma((subs,)),
            dma((subs,)),
            dma((crew,)),
            dma((crew,)),
            dma((everyone,)),
            dma((everyone,)),
            pltpu.SemaphoreType.REGULAR((max(cells - 1, 1), 2)),
        ],
        compiler_params=pltpu.CompilerParams(
            collective_id=0, has_side_effects=True, vmem_limit_bytes=16 * 1024 * 1024
        ),
    )(
        node_weights,
        *(pltpu.with_memory_space_constraint(array, pltpu.HBM) for array in (
            to_rows(adjoint_start),
            cell_points,
            neighbours,
            base_points,
            off_rows,
            to_rows(adjoint_rhs),
            inv_rows,
            sens_cells,
            ffd_index.T,
            ffd_weight.T,
        ))
    )
    adjoint, control = pl.pallas_call(
        finish,
        out_shape=(
            jax.ShapeDtypeStruct((5, rows, LANES), f32),
            jax.ShapeDtypeStruct((3, FFD), f32),
        ),
        in_specs=[vmem] * 2,
        out_specs=(vmem, vmem),
        compiler_params=pltpu.CompilerParams(vmem_limit_bytes=1024 * 1024),
    )(adjoint, control)
    return from_rows(adjoint, nodes_here), control


def solution(mesh):
    return jax.shard_map(
        body,
        mesh=mesh,
        in_specs=(
            P("nodes", None, ("groups", "cells", "sub")),
            P("nodes", None, ("groups", "cells", "sub")),
            P("nodes", None, None, ("groups", "cells", "sub")),
            P("nodes", None, ("groups", "cells", "sub")),
            P(None, ("cells", "sub")),
            P("nodes"),
            P("nodes", None, ("groups", "cells", "sub")),
            P(None, ("cells", "sub")),
            P(),
            P(),
            P(),
        ),
        out_specs=(P("nodes", None, ("groups", "cells", "sub")), P("groups", None)),
        check_vma=False,
    )
```
